32 devices in a mesh: grp: 2 (over y), seq: 4 (over z), head: 2 (over x), rep: 2 (over core).
Axes of the slice: x: 2, y: 2, z: 4, core: 2. Of those that a mesh axis runs over, the one named last changes fastest.
Arguments:
- tokens: bfloat16 [4096, 2048], P(('grp', 'seq'), 'rep'), parts along dimension 0, may hold values from -30 to 30, as said below
- projection: bfloat16 [2048, 3, 2048], P('rep', None, 'head'), may hold values from -0.116009706 to 0.116009706, as said below
- rand_table: int32 [16, 32, 3], P(('head', 'rep')), may hold values from 2 to 6
- round_masks: int32 [3], replicated, may hold values from 1 to 3, as said below
Outputs:
- context: bfloat16 [4096, 2048], P(('grp', 'seq'), ('head', 'rep')), parts along dimension 0
The draws below stay inside these ranges and needn't reach their ends.
There are 2 independent parts, one for each index of `grp`. The reference program is written for one: setup_inputs(seed, part) draws one part's arguments, and reference() takes and returns one part's arrays. A program takes and returns all parts, laid end to end along the dimension named above; an argument that names none is the same for every part. Nothing has to cross between parts.
Inputs may be any that keep to these rules, and one draw needn't show every extreme that they name: `tokens`: floats of the inputs; a few rows may be larger than the rest. `projection`: query and key columns are scaled a little above the fan-in rule. 3 distinct values; in round r shard i is paired with shard i xor round_masks[r]; one of them is 3. `rand_table`: an entry names a block inside the partner shard, never its first two nor its last.
All inputs are finite; a program needn't handle non-finite values.
Results may differ from the reference program's by a relative error of at most 0.0011.
The reference program's roundings to bfloat16 on the way count: a program that leaves them out, or rounds other values in their place, can miss the bound.
Values may be sent and summed in bfloat16 or wider, within the bound.
A program may use at most 128 MiB of HBM per device.

```python
import jax
import jax.numpy as jnp
from jax import lax

D = 2048
H = 16
HD = 128
B = 64
R = 3
SHARDS = 4
TOKENS = 2048
BPS = 8
NBLK = 32
HH = 2048


def draw_tokens(key, part):
    base = jnp.clip(jax.random.normal(key, (TOKENS, D), jnp.float32), -5.0, 5.0)
    result = base * 4.0
    return result.astype(jnp.bfloat16)


def draw_projection(key, part):
    first_key = jax.random.fold_in(key, 11)
    base = jnp.clip(jax.random.normal(first_key, (D, 3, HH), jnp.float32), -3.5, 3.5)
    factors = jnp.array([1.48, 1.48, 0.25], jnp.float32) / D ** 0.5
    result = base * factors[None, :, None]
    return result.astype(jnp.bfloat16)


def draw_round_masks(key, part):
    order_key = jax.random.fold_in(key, 5)
    place_key = jax.random.fold_in(key, 7)
    values = jax.random.permutation(order_key, SHARDS - 1) + 1
    top_place = jnp.argmax(values)
    chosen = values[:R]
    place = jax.random.randint(place_key, (), 0, R)
    chosen = jnp.where(top_place >= R, chosen.at[place].set(SHARDS - 1), chosen)
    return chosen.astype(jnp.int32)


def plant(values, rng, least, high):
    extent = values.shape
    spot = [jax.random.randint(jax.random.fold_in(rng, axis), (), 0, extent[axis]) for axis in range(len(extent))]
    values = values.at[tuple(spot)].set(least)
    longest = extent.index(max(extent))
    spot[longest] = (spot[longest] + 1) % extent[longest]
    return values.at[tuple(spot)].set(high)


def setup_inputs(seed: int = 0, part: int = 0) -> dict:
    keys = jax.random.split(jax.random.key(seed), 5)
    part_keys = jax.random.split(jax.random.fold_in(keys[4], part), 5)
    return {
        "tokens": draw_tokens(jax.random.fold_in(jax.random.fold_in(keys[4], part), 71), part),
        "projection": draw_projection(jax.random.fold_in(keys[4], 71), part),
        "rand_table": plant(jax.random.randint(keys[2], (H, NBLK, R), 2, BPS - 1), jax.random.fold_in(keys[2], 1), 2, (BPS - 1) - 1).astype(jnp.int32),
        "round_masks": draw_round_masks(jax.random.fold_in(keys[4], 71), part),
    }


def window_allowed():
    block_ids = jnp.arange(NBLK, dtype=jnp.int32)
    nearby = block_ids[:, None] - 1 + jnp.arange(3, dtype=jnp.int32)[None, :]
    allowed = (nearby >= 2) & (nearby < NBLK)
    allowed = jnp.repeat(allowed, B, axis=1)
    return jnp.concatenate([allowed, jnp.ones((NBLK, (2 + R) * B), dtype=bool)], axis=1)


def gather_keys(flat_rows, table_head, round_masks):
    blocked = flat_rows.reshape(NBLK, B, HD)
    zero_block = jnp.zeros((1, B, HD), flat_rows.dtype)
    padded = jnp.concatenate([zero_block, blocked, zero_block], axis=0)
    window_part = jnp.concatenate([padded[0:NBLK], padded[1:NBLK + 1], padded[2:NBLK + 2]], axis=1)
    global_part = jnp.broadcast_to(flat_rows[:2 * B][None], (NBLK, 2 * B, HD))
    block_ids = jnp.arange(NBLK, dtype=jnp.int32)
    partner = jnp.bitwise_xor((block_ids // BPS)[:, None], round_masks[None, :].astype(jnp.int32))
    source = (partner * BPS + table_head.astype(jnp.int32)).astype(jnp.int32)
    random_part = blocked[source].reshape(NBLK, R * B, HD)
    return jnp.concatenate([window_part, global_part, random_part], axis=1)


def reference(tokens, projection, rand_table, round_masks):
    scale = HD ** -0.5
    mixed_rows = jnp.dot(tokens, projection.reshape(D, 3 * H * HD), preferred_element_type=jnp.float32).astype(jnp.bfloat16)
    mixed_rows = mixed_rows.reshape(TOKENS, 3, H, HD).transpose(1, 2, 0, 3)
    allowed = window_allowed()

    def one_head(inputs):
        queries, key_rows, value_rows, table_head = inputs
        all_keys = gather_keys(key_rows, table_head, round_masks)
        all_values = gather_keys(value_rows, table_head, round_masks)
        blocked_queries = queries.reshape(NBLK, B, HD)
        scores = jnp.einsum('gqe,gke->gqk', blocked_queries.astype(jnp.float32), all_keys.astype(jnp.float32), precision=lax.Precision.HIGHEST) * scale
        scores = jnp.where(allowed[:, None, :], scores, -jnp.inf)
        peak = jnp.max(scores, axis=-1, keepdims=True)
        expd = jnp.exp(scores - peak)
        row_total = jnp.sum(expd, axis=-1, keepdims=True)
        weights = expd.astype(jnp.bfloat16)
        regular = jnp.einsum('gqk,gke->gqe', weights.astype(jnp.float32), all_values.astype(jnp.float32), precision=lax.Precision.HIGHEST) / row_total
        gscores = jnp.dot(queries[:2 * B].astype(jnp.float32), key_rows.astype(jnp.float32).T, precision=lax.Precision.HIGHEST) * scale
        gpeak = jnp.max(gscores, axis=-1, keepdims=True)
        gexp = jnp.exp(gscores - gpeak)
        gtotal = jnp.sum(gexp, axis=-1, keepdims=True)
        gacc = jnp.dot(gexp, value_rows.astype(jnp.float32), precision=lax.Precision.HIGHEST)
        rows_out = regular.reshape(TOKENS, HD)
        rows_out = rows_out.at[:2 * B].set(gacc / gtotal)
        return rows_out.astype(jnp.bfloat16)

    per_head = lax.map(one_head, (mixed_rows[0], mixed_rows[1], mixed_rows[2], rand_table))
    return per_head.transpose(1, 0, 2).reshape(TOKENS, H * HD)
```

```python
import functools

import jax
import jax.numpy as jnp
from jax import lax
from jax.experimental import pallas as pl
from jax.experimental.pallas import tpu as pltpu
from jax.sharding import PartitionSpec as P

HD = 128
B = 64
R = 3


def with_halo(block, sides, width):
    for axis, dim in sides:
        count = lax.axis_size(axis)
        forward = [(i, i + 1) for i in range(count - 1)]
        backward = [(target, source) for source, target in forward]
        low = lax.ppermute(
            lax.slice_in_dim(block, block.shape[dim] - width, None, axis=dim), axis, forward
        )
        high = lax.ppermute(lax.slice_in_dim(block, 0, width, axis=dim), axis, backward)
        block = jnp.concatenate([low, block, high], axis=dim)
    return block


def spread(shard, axis, root):
    mine = lax.axis_index(axis) == root
    return lax.psum(jnp.where(mine, shard, jnp.zeros_like(shard)), axis)


def from_partner(block, axis, apart):
    count = lax.axis_size(axis)
    route = []
    for low in range(count):
        high = low | 1 << apart
        if high != low and high < count:
            route += [(low, high), (high, low)]
    return lax.ppermute(block, axis, route)


def combined_all(part, axis, combine):
    gathered = jax.tree.map(lambda a: lax.all_gather(a, axis), part)

    def take(source):
        return jax.tree.map(lambda a: lax.dynamic_index_in_dim(a, source, 0, False), gathered)

    return lax.fori_loop(
        1, lax.axis_size(axis), lambda source, state: combine(state, take(source)), take(0)
    )


def combine_parts(former, latter):
    peak = jnp.maximum(former[0], latter[0])
    former_scale = jnp.exp(former[0] - peak)
    latter_scale = jnp.exp(latter[0] - peak)
    summed = former[1] * former_scale + latter[1] * latter_scale
    accum = former[2] * former_scale[..., None] + latter[2] * latter_scale[..., None]
    return (peak, summed, accum)


def take_blocks(source, indices):
    return jnp.take(source, indices, axis=1)


def bit_set(mask_value, bit_pos):
    return jnp.bitwise_and(jnp.right_shift(mask_value, bit_pos), 1) == 1


def body(tokens, projection, rand_table, round_masks):
    scale = HD ** (-0.5)
    tok_count = tokens.shape[0]
    width_local = tokens.shape[1]
    heads_group = projection.shape[2] // HD
    heads_here = heads_group // lax.axis_size("rep")
    blocks_here = tok_count // B
    shaped = projection.reshape(width_local, 3, heads_group, HD)
    summed = lax.psum_scatter(
        jnp.einsum("td,dshe->htse", tokens, shaped, preferred_element_type=jnp.float32),
        "rep",
        scatter_dimension=0,
        tiled=True,
    )
    mixed_rows = summed.astype(jnp.bfloat16)
    queries = mixed_rows[:, :, 0]
    key_vals = jnp.moveaxis(mixed_rows[:, :, 1:], 2, 0)
    shard_id = lax.axis_index("seq")
    shards = lax.axis_size("seq")
    total_blocks = shards * blocks_here
    padded = with_halo(key_vals, (("seq", 2),), B)
    window = jnp.stack(
        [
            padded[:, :, offset * B : offset * B + tok_count].reshape(
                2, heads_here, blocks_here, B, HD
            )
            for offset in range(3)
        ],
        axis=3,
    )
    window = window.reshape(2, heads_here, blocks_here, 3 * B, HD)
    lead_queries, lead_keys = (
        spread(queries[:, : 2 * B], "seq", 0),
        spread(key_vals[:, :, : 2 * B], "seq", 0),
    )
    global_part = jnp.broadcast_to(lead_keys[:, :, None], (2, heads_here, blocks_here, 2 * B, HD))
    blocked = key_vals.reshape(2, heads_here, blocks_here, B, HD)
    bit_count = shards.bit_length() - 1
    fetched = []
    for round_id in range(R):
        peer = jnp.bitwise_xor(shard_id, round_masks[round_id])
        wanted = lax.dynamic_slice_in_dim(
            rand_table[:, :, round_id], peer * blocks_here, blocks_here, 1
        )
        payload = jax.vmap(take_blocks, in_axes=(1, 0), out_axes=1)(blocked, wanted)
        for bit_pos in range(bit_count):
            swapped = from_partner(payload, "seq", bit_pos)
            payload = jnp.where(bit_set(round_masks[round_id], bit_pos), swapped, payload)
        fetched.append(payload)
    random_part = jnp.concatenate(fetched, axis=3)
    all_keys = jnp.concatenate([window, global_part, random_part], axis=3)
    block_ids = shard_id * blocks_here + jnp.arange(blocks_here, dtype=jnp.int32)
    nearby = block_ids[:, None] - 1 + jnp.arange(3, dtype=jnp.int32)[None, :]
    allowed = (nearby >= 2) & (nearby < total_blocks)
    allowed = jnp.repeat(allowed, B, axis=1)
    allowed = jnp.concatenate([allowed, jnp.ones((blocks_here, (2 + R) * B), dtype=bool)], axis=1)
    blocked_queries = queries.reshape(heads_here, blocks_here, B, HD)
    scores = (
        jnp.einsum(
            "hjqe,hjke->hjqk", blocked_queries, all_keys[0], preferred_element_type=jnp.float32
        )
        * scale
    )
    scores = jnp.where(allowed[None, :, None, :], scores, -jnp.inf)
    peak = jnp.max(scores, axis=-1, keepdims=True)
    expd = jnp.exp(scores - peak)
    row_total = jnp.sum(expd, axis=-1, keepdims=True)
    weights = expd.astype(jnp.bfloat16)
    regular = jnp.einsum(
        "hjqk,hjke->jqhe", weights, all_keys[1], preferred_element_type=jnp.float32
    )
    regular = regular / jnp.moveaxis(row_total, 0, 2)
    regular = regular.reshape(tok_count, heads_here, HD)
    gscores = (
        jnp.einsum("hqe,hke->hqk", lead_queries, key_vals[0], preferred_element_type=jnp.float32)
        * scale
    )
    local_peak = jnp.max(gscores, axis=-1)
    local_exp = jnp.exp(gscores - local_peak[..., None])
    local_sum = jnp.sum(local_exp, axis=-1)
    local_acc = jnp.einsum(
        "hqk,hke->hqe", local_exp, key_vals[1].astype(jnp.float32), precision=lax.Precision.HIGHEST
    )
    merged = combined_all((local_peak, local_sum, local_acc), "seq", combine_parts)
    global_rows = jnp.transpose(merged[2] / merged[1][..., None], (1, 0, 2))
    global_full = jnp.pad(global_rows, ((0, tok_count - 2 * B), (0, 0), (0, 0)))
    row_ids = jnp.arange(tok_count)
    use_global = (shard_id == 0) & (row_ids < 2 * B)
    combined = jnp.where(use_global[:, None, None], global_full, regular)
    return combined.reshape(tok_count, heads_here * HD).astype(jnp.bfloat16)


MESH = pl.DeviceIdType.MESH
DEPTH = 2 * B
OWNER = 0
X_LAG = 4
C_LAG = 7
LOG2E = 1.4426950408889634
CONTRACT = (((1,), (1,)), ((), ()))


def layer_kernel(
    shards, tok_ref, w_ref, q_s, k_s, v_s, full, wfull,
    zsend, zrecv, xsend, xrecv, csend, crecv, wsend, wrecv, lsem,
):
    s, x, c = lax.axis_index("seq"), lax.axis_index("head"), lax.axis_index("rep")
    rows, width = tok_ref.shape
    cols = width // 2
    mine = w_ref.shape[2] // 2
    heads = mine // HD
    blocks = rows // B
    steps = (shards - 1) * blocks
    has_up, has_down = s < shards - 1, s > 0
    up, down = {"seq": s + 1}, {"seq": s - 1}
    across, core = {"head": 1 - x}, {"rep": 1 - c}

    barrier = pltpu.get_barrier_semaphore()

    def greet(device):
        pl.semaphore_signal(barrier, inc=1, device_id=device, device_id_type=MESH)

    greet(across)
    greet(core)

    @pl.when(has_up)
    def _():
        greet(up)

    @pl.when(has_down)
    def _():
        greet(down)

    pl.semaphore_wait(barrier, 2 + has_up.astype(jnp.int32) + has_down.astype(jnp.int32))

    def remote(src, dst, send, recv, device):
        return pltpu.make_async_remote_copy(
            src_ref=src, dst_ref=dst, send_sem=send, recv_sem=recv, device_id=device, device_id_type=MESH
        )

    def rows_of(i, size=B):
        return pl.ds(pl.multiple_of(i * size, size), size)

    def quarter(i):
        return pl.ds(pl.multiple_of(c * width + i * cols, cols), cols)

    def half(i):
        return pl.ds(pl.multiple_of(i * width, width), width)

    def drawable(b):
        return (b >= 2) & (b < blocks - 1)

    def goes_up(at, src, b):
        return drawable(b) | ((b < 2) & (src == 0)) | ((b == blocks - 1) & (src == at))

    def goes_down(at, src, b):
        return drawable(b) | ((b == 0) & (src == at)) | (at > OWNER)

    def own_z(i, way):
        piece = tok_ref.at[rows_of(i), pl.ds(pl.multiple_of(x * cols, cols), cols)]
        return remote(piece, full.at[s, rows_of(i), quarter(x)], zsend.at[way, s, i], zrecv.at[s, i], (down, up)[way])

    def relay_z(src, i, way):
        piece = full.at[src, rows_of(i), quarter(x)]
        return remote(piece, piece, zsend.at[way, src, i], zrecv.at[src, i], (down, up)[way])

    def relay_x(src, i, which):
        piece = full.at[src, rows_of(i), quarter(which)]
        return remote(piece, piece, xsend.at[src, i], xrecv.at[src, i], across)

    def relay_c(src, i, which):
        piece = full.at[src, rows_of(i), half(which)]
        return remote(piece, piece, csend.at[src, i], crecv.at[src, i], core)

    def own_c(which):
        return remote(tok_ref, full.at[s, :, half(which)], wsend.at[3], wrecv.at[3], core)

    def weight_c(i, which):
        theirs = w_ref.at[i, :, pl.ds(pl.multiple_of((1 - c) * mine, mine), mine)]
        return remote(theirs, wfull.at[i, half(which), :], wsend.at[i], wrecv.at[i], core)

    def weight_l(i):
        own = w_ref.at[i, :, pl.ds(pl.multiple_of(c * mine, mine), mine)]
        return pltpu.make_async_copy(own, wfull.at[i, half(c), :], lsem.at[i])

    own_l = pltpu.make_async_copy(tok_ref, full.at[s, :, half(c)], lsem.at[3])

    def own_sends(act):
        def one(i, carry):
            @pl.when(has_up & goes_up(s, s, i))
            def _():
                act(own_z(i, 1))

            @pl.when(has_down & goes_down(s, s, i))
            def _():
                act(own_z(i, 0))

            return carry

        lax.fori_loop(0, blocks, one, 0)

    own_sends(lambda copy: copy.start())
    own_l.start()
    own_c(c).start()
    for i in (1, 2, 0):
        weight_c(i, c).start()
        weight_l(i).start()

    def product(src, pair, which):
        block = full[src, rows_of(pair, DEPTH), :]
        return jnp.dot(block, wfull[which], preferred_element_type=jnp.float32).astype(jnp.bfloat16)

    def put(dest, start, result):
        for h in range(heads):
            dest[h, pl.ds(pl.multiple_of(start, DEPTH), DEPTH), :] = result[:, h * HD:(h + 1) * HD]

    def project(src, pair):
        start = src * rows + pair * DEPTH
        put(k_s, start, product(src, pair, 1))
        put(v_s, start, product(src, pair, 2))

    def from_below(t, act):
        src, b = s - t // blocks - 1, t % blocks

        @pl.when((t >= 0) & (t < steps) & (src >= 0) & goes_up(s - 1, src, b))
        def _():
            act(src, b)

    def from_above(t, act):
        src, b = s + t // blocks + 1, t % blocks

        @pl.when((t >= 0) & (t < steps) & (src < shards) & goes_down(s + 1, src, b))
        def _():
            act(src, b)

    def pass_up(src, b, act):
        @pl.when(has_up & goes_up(s, src, b))
        def _():
            act(relay_z(src, b, 1))

    def pass_down(src, b, act):
        @pl.when(has_down & goes_down(s, src, b))
        def _():
            act(relay_z(src, b, 0))

    def take_z(passing):
        def act(src, b):
            relay_z(src, b, 0).wait_recv()
            passing(src, b, lambda copy: copy.start())
            relay_x(src, b, x).start()

        return act

    def take_x(src, b):
        relay_x(src, b, 1 - x).wait_recv()
        relay_c(src, b, c).start()

    def take_c(src, b):
        relay_c(src, b, 1 - c).wait_recv()

    def pairs(t):
        b = t % blocks
        whole = (t >= 0) & (t < steps) & (b % 2 == 1)
        low, high = s - t // blocks - 1, s + t // blocks + 1

        @pl.when(whole & (low >= 0) & ((b > 1) | (low == 0)))
        def _():
            project(low, b // 2)

        @pl.when(whole & (high < shards) & ((b > 1) | (high == s + 1) | (s >= OWNER)))
        def _():
            project(high, b // 2)

    def step(t, carry):
        from_below(t, take_z(pass_up))
        from_above(t, take_z(pass_down))
        from_below(t - X_LAG, take_x)
        from_above(t - X_LAG, take_x)

        @pl.when(t == 5)
        def _():
            own_l.wait()
            own_c(1 - c).wait_recv()
            for i in range(3):
                weight_l(i).wait()
                weight_c(i, 1 - c).wait_recv()

        @pl.when((t >= 5) & (t < 5 + blocks // 2))
        def _():
            project(s, t - 5)
            put(q_s, (t - 5) * DEPTH, product(s, t - 5, 0))

        from_below(t - C_LAG, take_c)
        from_above(t - C_LAG, take_c)
        pairs(t - C_LAG)
        return carry

    lax.fori_loop(0, steps + C_LAG, step, 0)

    own_c(c).wait_send()
    for i in range(3):
        weight_c(i, c).wait_send()
    own_sends(lambda copy: copy.wait_send())

    def sent(passing):
        def act(src, b):
            passing(src, b, lambda copy: copy.wait_send())
            relay_x(src, b, x).wait_send()
            relay_c(src, b, c).wait_send()

        return act

    def drain(t, carry):
        from_below(t, sent(pass_up))
        from_above(t, sent(pass_down))
        return carry

    lax.fori_loop(0, steps, drain, 0)


def attend_kernel(blocks, table_ref, mask_ref, q_ref, k_ref, v_ref, o_ref):
    h = pl.program_id(0)
    s = lax.axis_index("seq")
    total = k_ref.shape[1] // B
    scale = HD ** (-0.5)

    def rows_of(i):
        return pl.ds(pl.multiple_of(i * B, B), B)

    def picks(j):
        g = s * blocks + j
        chosen = [jnp.clip(g + d, 0, total - 1) for d in (-1, 0, 1)] + [0, 1]
        for r in range(R):
            chosen.append(jnp.bitwise_xor(s, mask_ref[r]) * blocks + table_ref[r, h, g])
        return chosen

    def taken(ref, j):
        return jnp.concatenate([ref[0, rows_of(p), :] for p in picks(j)], axis=0)

    def softmax(scores):
        expd = jnp.exp2((scores - jnp.max(scores, axis=-1, keepdims=True)) * (scale * LOG2E))
        return expd, 1.0 / jnp.sum(expd, axis=-1, keepdims=True)

    lane = lax.broadcasted_iota(jnp.int32, (1, 2 * B), 1)
    scores = [
        lax.dot_general(q_ref[0, j * B:(j + 1) * B, :], taken(k_ref, j), CONTRACT, preferred_element_type=jnp.float32)
        for j in range(blocks)
    ]
    weights, inverse = [], []
    for j in range(blocks):
        near = [s * blocks + j + d for d in (-1, 0, 1)]
        below, here, above = [jnp.where((n >= 2) & (n < total), 0.0, -jnp.inf) for n in near]
        masked = [
            scores[j][:, :2 * B] + jnp.where(lane < B, below, here),
            scores[j][:, 2 * B:4 * B] + jnp.where(lane < B, above, 0.0),
            scores[j][:, 4 * B:],
        ]
        expd, over = softmax(jnp.concatenate(masked, axis=1))
        weights.append(expd.astype(jnp.bfloat16))
        inverse.append(over)
    for j in range(blocks):
        out = jnp.dot(weights[j], taken(v_ref, j), preferred_element_type=jnp.float32)
        o_ref[j * B:(j + 1) * B, :] = (out * inverse[j]).astype(jnp.bfloat16)

    @pl.when(s == 0)
    def _():
        scores = lax.dot_general(q_ref[0, :DEPTH, :], k_ref[0], CONTRACT, preferred_element_type=jnp.float32)
        expd, over = softmax(scores)
        high = expd.astype(jnp.bfloat16)
        low = (expd - high.astype(jnp.float32)).astype(jnp.bfloat16)
        values = v_ref[0]
        accum = jnp.dot(high, values, preferred_element_type=jnp.float32)
        accum += jnp.dot(low, values, preferred_element_type=jnp.float32)
        o_ref[:DEPTH, :] = (accum * over).astype(jnp.bfloat16)


def gathered_body(shards, tokens, projection, rand_table, round_masks):
    rows, width = tokens.shape
    mine = projection.shape[2] // 2
    heads = mine // HD
    blocks = rows // B
    dma = pltpu.SemaphoreType.DMA
    bf16 = jnp.bfloat16
    smem = pl.BlockSpec(memory_space=pltpu.SMEM)
    hbm = pl.BlockSpec(memory_space=pltpu.HBM)
    lengths = (rows, shards * rows, shards * rows)
    parts = pl.pallas_call(
        functools.partial(layer_kernel, shards),
        out_shape=tuple(jax.ShapeDtypeStruct((heads, length, HD), bf16) for length in lengths),
        in_specs=[hbm, hbm],
        out_specs=[pl.BlockSpec(memory_space=pltpu.VMEM)] * 3,
        scratch_shapes=[
            pltpu.VMEM((shards, rows, 2 * width), bf16),
            pltpu.VMEM((3, 2 * width, mine), bf16),
            dma((2, shards, blocks)),
            dma((shards, blocks)),
            dma((shards, blocks)),
            dma((shards, blocks)),
            dma((shards, blocks)),
            dma((shards, blocks)),
            dma((4,)),
            dma((4,)),
            dma((4,)),
        ],
        compiler_params=pltpu.CompilerParams(
            collective_id=0, has_side_effects=True, vmem_limit_bytes=48 * 1024 * 1024
        ),
        name="gather_project",
    )(tokens, jnp.transpose(projection, (1, 0, 2)))
    return pl.pallas_call(
        functools.partial(attend_kernel, blocks),
        out_shape=jax.ShapeDtypeStruct((rows, mine), bf16),
        grid=(heads,),
        in_specs=[smem, smem] + [pl.BlockSpec((1, length, HD), lambda h: (h, 0, 0)) for length in lengths],
        out_specs=pl.BlockSpec((rows, HD), lambda h: (0, h)),
        compiler_params=pltpu.CompilerParams(vmem_limit_bytes=12 * 1024 * 1024),
        name="attend",
    )(jnp.transpose(rand_table, (2, 0, 1)), round_masks, *parts)


def solution(mesh):
    shards = mesh.shape["seq"]
    few = shards == R + 1 and mesh.shape["head"] == 2
    return jax.shard_map(
        functools.partial(gathered_body, shards) if few else body,
        mesh=mesh,
        in_specs=(
            P(("grp", "seq"), "rep"),
            P("rep", None, "head"),
            P(("head", "rep"), None, None),
            P(),
        ),
        out_specs=P(("grp", "seq"), ("head", "rep")),
        check_vma=False,
    )
```
